32 devices in a mesh: tm: 4 (over y, x), space: 8 (over z, core).
Axes of the slice: x: 2, y: 2, z: 4, core: 2. Of those that a mesh axis runs over, the one named last changes fastest.
Arguments:
- forcing: float32 [4, 64, 16384], P('tm', 'space'), may hold values from -6 to 6
- conductivity: float32 [64, 16384], P('space'), may hold values from 0.1 to 1
Outputs:
- solution: float32 [4, 64, 16384], P('tm', 'space')
The draws below stay inside these ranges and needn't reach their ends.
All inputs are finite; a program needn't handle non-finite values.
Results may differ from the reference program's by a relative error of at most 0.0001.
Values sent between devices are 32-bit elements; how exact they have to be, the bound alone decides.
A program may use at most 64 MiB of HBM per device.

```python
import math
import jax
import jax.numpy as jnp

NY = 16384
ITERS = 3
NT = 4
NX = 64


def block_scale(stream_key, dims, shards, low, high):
    gain = 1.0
    for axis_at, blocks in shards:
        steps = jax.random.uniform(jax.random.fold_in(jax.random.fold_in(stream_key, 6), axis_at), (blocks,), jnp.float32, low / len(shards), high / len(shards))
        gain = gain * jnp.repeat(jnp.exp(steps), dims[axis_at] // blocks).reshape((-1,) + (1,) * (len(dims) - 1 - axis_at))
    return gain


def centred(key, dims, spread, most, split=(), kind=jnp.bfloat16):
    factor_of = block_scale(key, dims, split, -0.22, 0.18) if split else 1.0
    drawn = jax.random.normal(key, dims, jnp.float32) * spread * factor_of
    return jnp.minimum(jnp.maximum(drawn, -most), most).astype(kind)


def setup_inputs(seed: int = 0) -> dict:
    key_list = jax.random.split(jax.random.key(seed), 3)
    return {
        "forcing": centred(key_list[0], (NT, NX, NY), 1.0, 6.0, ((0, 4), (1, 8)), jnp.float32),
        "conductivity": jnp.clip(jnp.exp(math.log(1.0) - 2.3025851 * jax.random.uniform(key_list[1], (NX, NY), jnp.float32) ** block_scale(key_list[1], (NX, NY), ((0, 8),), -0.2, 0.2)), 0.1, 1.0),
    }


def edge_weights(kpad):
    center = kpad[1:-1, 1:-1]
    north = 0.5 * (center + kpad[:-2, 1:-1])
    south = 0.5 * (center + kpad[2:, 1:-1])
    west = 0.5 * (center + kpad[1:-1, :-2])
    east = 0.5 * (center + kpad[1:-1, 2:])
    diag = 1.0 + north + south + west + east
    return (north, south, west, east, diag)

def neighbours(field, north, south, west, east):
    padded = jnp.pad(field, ((0, 0), (1, 1), (1, 1)))
    total = north * padded[:, :-2, 1:-1] + south * padded[:, 2:, 1:-1]
    return total + west * padded[:, 1:-1, :-2] + east * padded[:, 1:-1, 2:]

def operate(field, weights):
    north, south, west, east, diag = weights
    stepped = diag * field - neighbours(field, north, south, west, east)
    earlier = jnp.concatenate([jnp.zeros_like(field[:1]), field[:-1]], 0)
    return jnp.flip(stepped - earlier, 0)

def precondition(field, weights, scale):
    north, south, west, east, diag = weights

    def apply_g(term):
        return scale * neighbours(scale * term, north, south, west, east)
    first = scale * field
    second = apply_g(first)
    third = 2.0 * apply_g(second) - first
    fourth = 2.0 * apply_g(third) - second
    return scale * (first + 0.5 * second + 0.25 * third + 0.125 * fourth)

def reference(forcing, conductivity):
    weights = edge_weights(jnp.pad(conductivity, 1))
    scale = 1.0 / jnp.sqrt(weights[4])
    vec = jnp.flip(forcing, 0)
    vec_old = jnp.zeros_like(vec)
    zvec = precondition(vec, weights, scale)
    gamma = jnp.sqrt(jnp.sum(zvec * vec))
    gamma_old = jnp.float32(1.0)
    wvec = jnp.zeros_like(vec)
    wvec_old = jnp.zeros_like(vec)
    solution = jnp.zeros_like(vec)
    cos_now = jnp.float32(1.0)
    cos_old = jnp.float32(1.0)
    sin_now = jnp.float32(0.0)
    sin_old = jnp.float32(0.0)
    eta = gamma
    for step in range(ITERS):
        zvec = zvec / gamma
        image = operate(zvec, weights)
        delta = jnp.sum(image * zvec)
        vec_new = image - delta / gamma * vec - gamma / gamma_old * vec_old
        zvec_new = precondition(vec_new, weights, scale)
        gamma_new = jnp.sqrt(jnp.sum(zvec_new * vec_new))
        alpha_zero = cos_now * delta - cos_old * sin_now * gamma
        alpha_one = jnp.sqrt(alpha_zero * alpha_zero + gamma_new * gamma_new)
        alpha_two = sin_now * delta + cos_old * cos_now * gamma
        alpha_three = sin_old * gamma
        cos_new = alpha_zero / alpha_one
        sin_new = gamma_new / alpha_one
        wvec_new = (zvec - alpha_three * wvec_old - alpha_two * wvec) / alpha_one
        solution = solution + cos_new * eta * wvec_new
        eta = -sin_new * eta
        vec_old, vec, zvec = (vec, vec_new, zvec_new)
        gamma_old, gamma = (gamma, gamma_new)
        wvec_old, wvec = (wvec, wvec_new)
        cos_old, cos_now, sin_old, sin_now = (cos_now, cos_new, sin_now, sin_new)
    return solution
```

```python
import functools

import jax
import jax.numpy as jnp
from jax import lax
from jax.experimental import pallas as pl
from jax.experimental.pallas import tpu as pltpu
from jax.sharding import PartitionSpec as P

MESH = pl.DeviceIdType.MESH
LANES = 128
SUB = 8
ITERS = 3
SWEEPS = 4 * ITERS + 2


def kernel(
    ntm, nsp, reach, f_hbm, k_hbm, out_hbm,
    fstage, kloc, kstage, fwin, kwin, scl, inv, gn, gs, gw, ge, taus, abufs, bbufs, qs, last, res, part, red,
    f_sem, k_sem, r_sem, o_sem, own_sem,
):
    n = ntm * nsp
    mt, ms = lax.axis_index("tm"), lax.axis_index("space")
    me = mt * nsp + ms
    tl, nb, own, rows, _ = f_hbm.shape
    steps, width = fwin.shape[0], fwin.shape[1]
    strips = nsp // 2
    half, ml = ms // strips, ms % strips
    mb = mt * strips + ml
    nx = scl.shape[1] - 2 * SUB
    groups, owned = nx // SUB, strips * rows // SUB
    spare = groups - owned
    edge = jnp.where(half == 0, ml >= strips - reach, ml < reach)

    def place(s, side):
        at = s - side * (strips - reach)
        return pl.ds(pl.multiple_of(SUB + at * rows, SUB), rows)

    def send(src, dst, sem, arrival, dt, ds):
        return pltpu.make_async_remote_copy(
            src_ref=src, dst_ref=dst, send_sem=sem, recv_sem=arrival,
            device_id=(dt, ds), device_id_type=MESH)

    def f_copy(dt, side, dl):
        return send(fstage.at[:, dt * strips + dl],
                    fwin.at[pl.ds(mt * tl, tl), :, place(ms, side)],
                    f_sem.at[0], f_sem.at[1], dt, side * strips + dl)

    def f_cross(dt, side, dl):
        return send(fstage.at[:, dt * strips + dl],
                    fwin.at[pl.ds(mt * tl, tl), :, place(ms, side)],
                    f_sem.at[0], f_sem.at[2], dt, side * strips + dl)

    def k_copy(side, dl):
        return send(kstage.at[dl], kwin.at[:, place(ms, side)],
                    k_sem.at[0], k_sem.at[1], mt, side * strips + dl)

    def r_copy(dt, ds):
        return send(part, red.at[me], r_sem.at[0], r_sem.at[1], dt, ds)

    def res_piece(dt, dl):
        return res.at[pl.ds(dt * tl, tl), :, pl.ds(pl.multiple_of(dl * rows, SUB), rows)]

    def o_copy(dt, dl):
        return send(res_piece(dt, dl), out_hbm.at[:, pl.ds(mb * own, own)],
                    o_sem.at[0], o_sem.at[1], dt, half * strips + dl)

    def await_bytes(ref, sem):
        pltpu.make_async_copy(ref, ref, sem).wait()

    def loop(low, high, act):
        def step(j, carry):
            act(j)
            return carry
        lax.fori_loop(low, high, step, 0)

    def turn(at, by, size):
        moved = at + by
        return jnp.where(moved >= size, moved - size, moved)

    def peers(act):
        for js in sorted(range(nsp), key=lambda j: abs(j - nsp // 2)):
            ds = turn(ms, js, nsp)
            for jt in range(ntm):
                if js or jt:
                    act(turn(mt, jt, ntm), ds)

    def home(i):
        return 2 * turn(ml // 2, 1 + i // 2, strips // 2) + (ml + i) % 2

    def mates(act):
        for i in range(strips):
            for jt in range(ntm):
                if (i, jt) != (strips - 2, 0):
                    act(turn(mt, jt, ntm), half, home(i))

    def across(i):
        near = 2 * (i // 2)
        return jnp.where(half == 0, near, strips - 2 - near) + (ml + i) % 2

    def others(act):
        for i in range(strips):
            for jt in range(ntm):
                act(turn(mt, jt, ntm), 1 - half, across(i))

    barrier = pltpu.get_barrier_semaphore()
    peers(lambda dt, ds: pl.semaphore_signal(
        barrier, inc=1, device_id=(dt, ds), device_id_type=MESH))
    loads = [
        pltpu.make_async_copy(f_hbm, fstage.at[:, :, pl.ds(0, own)], own_sem.at[0]),
        pltpu.make_async_copy(k_hbm, kloc, own_sem.at[1]),
        pltpu.make_async_copy(
            k_hbm.at[pl.ds(mt * strips, strips)], kstage.at[:, pl.ds(0, own)], own_sem.at[2]),
    ]
    for load in loads:
        load.start()
    lane = lax.broadcasted_iota(jnp.int32, (SUB, LANES), 1)
    first, final, ahead = lane == 0, lane == LANES - 1, lane < LANES // 2

    def beside(d, right, left):
        return jnp.where(ahead, right * jnp.where(d < nb - 1, 1.0, 0.0),
                         left * jnp.where(d > 0, 1.0, 0.0))

    def after(d):
        return jnp.minimum(d + 1, nb - 1)

    def before(d):
        return jnp.maximum(d - 1, 0)

    for load in loads:
        load.wait()

    def interleave(act):
        by = 1
        while by < own:
            odd = (lane & by) != 0

            def swap(tiles, by=by, odd=odd):
                pairs = [(c, c + by) for c in range(own) if not c & by]
                got = [[(get(a), get(b)) for a, b in pairs] for get, _ in tiles]
                turned = [[(pltpu.roll(y, by, 1), pltpu.roll(x, LANES - by, 1)) for x, y in g] for g in got]
                for (_, put), g, h in zip(tiles, got, turned):
                    for (a, b), (x, y), (ry, rx) in zip(pairs, g, h):
                        put(a, jnp.where(odd, ry, x))
                        put(b, jnp.where(odd, y, rx))

            act(swap, by == 1)
            by *= 2

    def overlap_k(s):
        d = mt * strips + s
        for r in range(0, rows, SUB):
            kstage[s, own, r:r + SUB, :] = beside(
                d, kloc[after(d), 0, r:r + SUB, :], kloc[before(d), own - 1, r:r + SUB, :])

    def overlap_f(d):
        for t in range(tl):
            for r in range(0, rows, SUB):
                fstage[t, d, own, r:r + SUB, :] = beside(
                    d, fstage[t, after(d), 0, r:r + SUB, :],
                    fstage[t, before(d), own - 1, r:r + SUB, :])

    def cell(ref, *head, r=0):
        def get(c):
            return ref[(*head, c, pl.ds(r, SUB), slice(None))]

        def put(c, x):
            ref[(*head, c, pl.ds(r, SUB), slice(None))] = x
        return get, put

    batch = 4 if nb % 4 == 0 else 1
    bands = range(0, rows, SUB)

    def weave_k(swap, _):
        swap([cell(kstage, s, r=r) for s in range(strips) for r in bands])

    def weave_f(swap, _):
        loop(0, nb // batch, lambda j: swap(
            [cell(fstage, t, batch * j + d, r=r) for d in range(batch) for t in range(tl) for r in bands]))

    loop(0, strips, overlap_k)
    interleave(weave_k)
    loop(0, nb, overlap_f)
    interleave(weave_f)
    own_k = pltpu.make_async_copy(kstage.at[ml], kwin.at[:, place(ms, half)], k_sem.at[1])
    own_f = pltpu.make_async_copy(
        fstage.at[:, mb], fwin.at[pl.ds(mt * tl, tl), :, place(ms, half)], f_sem.at[1])
    zero = jnp.zeros((SUB, LANES), jnp.float32)
    rims = (slice(0, SUB), slice(SUB + nx, SUB + nx + SUB))

    def clear(c):
        for rim in rims:
            kwin[c, rim, :] = zero
            scl[c, rim, :] = zero
            for s in range(steps):
                last[s, c, rim, :] = zero
                for many in (taus, abufs, bbufs, qs):
                    for j in range(many.shape[0]):
                        many[j, s, c, rim, :] = zero

    loop(0, width, clear)
    pl.semaphore_wait(barrier, n - 1)

    for i in range(strips):
        if i != strips - 2:
            k_copy(half, home(i)).start()

    @pl.when(edge)
    def _():
        for i in range(strips):
            k_copy(1 - half, across(i)).start()

    mates(lambda *to: f_copy(*to).start())

    @pl.when(edge)
    def _():
        others(lambda *to: f_cross(*to).start())

    own_k.start()
    own_f.start()
    await_bytes(kwin.at[:, pl.ds(SUB, nx)], k_sem.at[1])

    def turned(x0, x1, rim):
        down, up = pltpu.roll(rim, 1, 1), pltpu.roll(rim, LANES - 1, 1)
        start = jnp.where(lane < own, pltpu.roll(x1, own + 1, 1), pltpu.roll(x1, own, 1))
        end = jnp.where(lane >= LANES - own,
                        pltpu.roll(x0, LANES - own - 1, 1), pltpu.roll(x0, LANES - own, 1))
        return (jnp.where(first, down, start), jnp.where(first, pltpu.roll(x1, 1, 1), down),
                jnp.where(final, up, end), jnp.where(final, pltpu.roll(x0, LANES - 1, 1), up))

    def lefts(xs):
        ends = turned(xs[0], xs[own - 1], xs[own])
        return [ends[0], *xs[:own - 1], ends[1]]

    def rights(xs):
        ends = turned(xs[0], xs[own - 1], xs[own])
        return [*xs[1:own], ends[2], ends[3]]

    def near(i, offset):
        return pl.ds(SUB + SUB * i + offset, SUB)

    def at(i):
        return pl.ds(pl.multiple_of(SUB + SUB * i, SUB), SUB)

    def flat(i):
        return pl.ds(pl.multiple_of(SUB * i, SUB), SUB)

    inside = beside(mb, jnp.ones((SUB, LANES), jnp.float32), jnp.ones((SUB, LANES), jnp.float32))

    def weights_first(i):
        ks = [kwin[c, at(i), :] for c in range(width)]
        for c, (k, l, r) in enumerate(zip(ks, lefts(ks), rights(ks))):
            up, down = kwin[c, near(i, -1), :], kwin[c, near(i, 1), :]
            diag = 1.0 + 0.5 * (k + up) + 0.5 * (k + down) + 0.5 * (k + l) + 0.5 * (k + r)
            scale = 1.0 / jnp.sqrt(diag)
            scl[c, at(i), :] = scale * inside if c == own else scale
            inv[c, flat(i), :] = 1.0 / diag

    def weights_second(i):
        ks = [kwin[c, at(i), :] for c in range(width)]
        ss = [scl[c, at(i), :] for c in range(width)]
        quads = zip(ks, lefts(ks), rights(ks), ss, lefts(ss), rights(ss))
        for c, (k, kl, kr, s, sl, sr) in enumerate(quads):
            half_s = 0.5 * s
            gn[c, flat(i), :] = half_s * (k + kwin[c, near(i, -1), :]) * scl[c, near(i, -1), :]
            gs[c, flat(i), :] = half_s * (k + kwin[c, near(i, 1), :]) * scl[c, near(i, 1), :]
            gw[c, flat(i), :] = half_s * (k + kl) * sl
            ge[c, flat(i), :] = half_s * (k + kr) * sr

    loop(0, groups, weights_first)
    loop(0, groups, weights_second)

    def group(j):
        return jnp.where(half == 0, j, groups - 1 - j)

    def scale_in(j):
        i = group(j)
        for c in range(width):
            s = scl[c, at(i), :]
            for t in range(steps):
                taus[0, t, c, at(i), :] = s * fwin[steps - 1 - t, c, at(i), :]

    def sweep(src, use, low, high, total):
        def block(j, total):
            i = group(j)
            ends = []
            for t in range(steps):
                ends.append(turned(src[t, 0, at(i), :], src[t, own - 1, at(i), :], src[t, own, at(i), :]))

            def beside_of(t, c):
                here = ends[t]
                left = here[0] if c == 0 else here[1] if c == own else src[t, c - 1, at(i), :]
                right = here[2] if c == own - 1 else here[3] if c == own else src[t, c + 1, at(i), :]
                return left, right

            for c in (*range(1, own - 1), 0, own - 1, own):
                wn, wso = gn[c, flat(i), :], gs[c, flat(i), :]
                ww, we = gw[c, flat(i), :], ge[c, flat(i), :]
                out = []
                for t in range(steps):
                    left, right = beside_of(t, c)
                    out.append(
                        wn * src[t, c, near(i, -1), :] + wso * src[t, c, near(i, 1), :]
                        + (ww * left + we * right))
                term = use(c, i, [src[t, c, at(i), :] for t in range(steps)], out)
                if term is not None and c < own:
                    total = total + term
            return total
        return lax.fori_loop(low, high, block, total)

    def one(it):
        def use(c, i, x, g):
            for t in range(steps):
                abufs[it, t, c, at(i), :] = x[t] + g[t]
        return taus.at[it], use

    def two(it):
        def use(c, i, x, g):
            for t in range(steps):
                bbufs[it, t, c, at(i), :] = 0.25 * taus[it, t, c, at(i), :] + g[t]
        return abufs.at[it], use

    def three(it):
        def use(c, i, x, g):
            term = zero
            for t in range(steps):
                v = taus[it, t, c, at(i), :]
                y = 1.5 * v + g[t]
                qs[it, t, c, at(i), :] = y
                term = term + v * y
            return term
        return bbufs.at[it], use

    def operate(it):
        def use(c, i, x, g):
            shrink = inv[c, flat(i), :]
            term = zero
            for t in range(steps):
                y = x[t] - g[t]
                if t:
                    y = y - shrink * x[t - 1]
                taus[it + 1, steps - 1 - t, c, at(i), :] = y
                term = term + y * x[steps - 1 - t]
            return term
        return qs.at[it], use

    def norm_one(c, i, x, g):
        term = zero
        for t in range(steps):
            last[t, c, at(i), :] = g[t]
            term = term + (x[t] * (1.5 * x[t] + 0.25 * g[t]) + g[t] * g[t])
        return term

    def norm_two(c, i, x, g):
        term = zero
        for t in range(steps):
            term = term + x[t] * g[t]
        return term

    plan = []
    for it in range(ITERS):
        plan += [(*one(it), None), (*two(it), None),
                 (*three(it), 2 * it - 1 if it else None), (*operate(it), 2 * it)]
    plan += [(taus.at[ITERS], norm_one, 2 * ITERS - 1), (last, norm_two, 2 * ITERS - 1)]
    moments = [zero] * (2 * ITERS)

    def run(number, low, middle, high):
        src, use, slot = plan[number - 1]
        if low < middle:
            base = zero if slot is None else moments[slot]
            total = sweep(src, use, low, middle, base)
            if slot is not None:
                moments[slot] = total
        if max(low, middle) < high:
            sweep(src, use, max(low, middle), high, zero)

    def up_to(count):
        return -(-count // SUB)

    inner = owned * SUB
    ready = [(inner - j) // SUB for j in range(SWEEPS + 1)]
    early = [max(up_to(SUB * ready[i] + i - j) for i in range(j, SWEEPS + 1))
             for j in range(SWEEPS + 1)]
    need = [owned + up_to(SWEEPS - j) for j in range(SWEEPS + 1)]

    await_bytes(fwin.at[:, :, pl.ds(SUB, inner)], f_sem.at[1])
    loop(0, owned, scale_in)
    for j in range(1, SWEEPS + 1):
        run(j, 0, ready[j], early[j])
    await_bytes(fwin.at[:, :, pl.ds(SUB, nx - inner)], f_sem.at[2])
    loop(owned, groups, scale_in)
    for j in range(1, SWEEPS + 1):
        run(j, ready[j], owned, need[j])

    row = jnp.zeros((1, LANES), jnp.float32)
    lane1 = lax.broadcasted_iota(jnp.int32, (1, LANES), 1)
    for j, m in enumerate(moments):
        value = jnp.sum(jnp.sum(m, axis=0, keepdims=True), axis=1, keepdims=True)
        row = jnp.where(lane1 == j, value, row)
    part[...] = row
    red[me] = row
    peers(lambda dt, ds: r_copy(dt, ds).start())

    def scaled(l, t, it, begin):
        i = l + half * spare

        def get(c):
            q = qs[it, t, c, at(i), :]
            return scl[c, at(i), :] * q if begin else q

        def put(c, x):
            qs[it, t, c, at(i), :] = x
        return get, put

    def unweave(swap, begin):
        loop(0, owned, lambda l: [
            swap([scaled(l, t, it, begin) for t in range(steps)]) for it in range(ITERS)] and None)

    interleave(unweave)
    await_bytes(red.at[pl.ds(0, n - 1)], r_sem.at[1])
    total = lax.fori_loop(0, n, lambda j, acc: acc + red[j], jnp.zeros((1, LANES), jnp.float32))
    n1, n2, n3, n4, n5, n6 = [
        jnp.sum(jnp.where(lane1 == j, total, 0.0), axis=1, keepdims=True) for j in range(6)]

    tiny = 1e-7
    d1 = jnp.maximum(n2, 1e-37)
    l21, l31 = n3 / d1, n4 / d1
    d2 = jnp.maximum(n4 - l21 * n3, jnp.maximum(tiny * n4, 1e-37))
    e32 = n5 - l31 * n3
    l32 = e32 / d2
    d3 = jnp.maximum(n6 - l31 * n4 - l32 * e32, jnp.maximum(tiny * n6, 1e-37))
    y2 = n2 - l21 * n1
    y3 = n3 - l31 * n1 - l32 * y2
    a2 = y3 / d3
    a1 = y2 / d2 - l32 * a2
    a0 = n1 / d1 - l21 * a1 - l31 * a2

    def finish(l):
        i = l + half * spare
        for c in range(own):
            for t in range(steps):
                res[t, c, flat(l), :] = (
                    a0 * qs[0, t, c, at(i), :] + a1 * qs[1, t, c, at(i), :]
                    + a2 * qs[2, t, c, at(i), :])

    own_out = pltpu.make_async_copy(
        res_piece(mt, ml), out_hbm.at[:, pl.ds(mb * own, own)], o_sem.at[1])
    for i in range(strips):
        dl = home(i)
        for r in range(rows // SUB):
            finish(dl * (rows // SUB) + r)
        for jt in range(ntm):
            if (i, jt) == (strips - 2, 0):
                own_out.start()
            else:
                o_copy(turn(mt, jt, ntm), dl).start()
    await_bytes(kstage.at[pl.ds(0, strips - 1)], k_sem.at[0])
    await_bytes(fstage.at[:, pl.ds(0, nb - 1)], f_sem.at[0])

    @pl.when(edge)
    def _():
        await_bytes(kstage, k_sem.at[0])
        await_bytes(fstage, f_sem.at[0])

    await_bytes(red.at[pl.ds(0, n - 1)], r_sem.at[0])
    await_bytes(out_hbm, o_sem.at[1])
    await_bytes(out_hbm.at[:, pl.ds(0, (nb - 1) * own)], o_sem.at[0])


def solution(mesh):
    ntm, nsp = mesh.shape["tm"], mesh.shape["space"]
    n, nb = ntm * nsp, ntm * (nsp // 2)

    def body(forcing, conductivity):
        tl, rows, columns = forcing.shape
        tiles = columns // LANES
        own = tiles // nb
        width = own + 1
        reach = -(-(SWEEPS + 1) // rows)
        steps, nx = tl * ntm, (nsp // 2 + reach) * rows
        f = forcing.reshape(tl, rows, nb, own, LANES).transpose(0, 2, 3, 1, 4)
        k = conductivity.reshape(rows, nb, own, LANES).transpose(1, 2, 0, 3)
        padded = pltpu.VMEM((width, nx + 2 * SUB, LANES), jnp.float32)
        plain = pltpu.VMEM((width, nx, LANES), jnp.float32)

        def fields(*many):
            return pltpu.VMEM((*many, steps, width, nx + 2 * SUB, LANES), jnp.float32)

        dma = pltpu.SemaphoreType.DMA
        f, k = (pltpu.with_memory_space_constraint(x, pltpu.HBM) for x in (f, k))
        out = pl.pallas_call(
            functools.partial(kernel, ntm, nsp, reach),
            out_shape=jax.ShapeDtypeStruct((tl, tiles, rows, LANES), jnp.float32),
            in_specs=[pl.BlockSpec(memory_space=pltpu.HBM)] * 2,
            out_specs=pl.BlockSpec(memory_space=pl.ANY),
            scratch_shapes=[
                pltpu.VMEM((tl, nb, width, rows, LANES), jnp.float32),
                pltpu.VMEM((nb, own, rows, LANES), jnp.float32),
                pltpu.VMEM((nsp // 2, width, rows, LANES), jnp.float32),
                fields(), padded, padded, plain, plain, plain, plain, plain,
                fields(ITERS + 1), fields(ITERS), fields(ITERS), fields(ITERS), fields(),
                pltpu.VMEM((steps, own, nsp // 2 * rows, LANES), jnp.float32),
                pltpu.VMEM((1, LANES), jnp.float32),
                pltpu.VMEM((n, 1, LANES), jnp.float32),
                dma((3,)), dma((2,)), dma((2,)), dma((2,)), dma((3,)),
            ],
            compiler_params=pltpu.CompilerParams(
                collective_id=0, has_side_effects=True, vmem_limit_bytes=40 * 1024 * 1024),
        )(f, k)
        return out.transpose(0, 2, 1, 3).reshape(tl, rows, columns)

    return jax.shard_map(
        body,
        mesh=mesh,
        in_specs=(P("tm", "space", None), P("space", None)),
        out_specs=P("tm", "space", None),
        check_vma=False,
    )
```

```python
import functools

import jax
import jax.numpy as jnp
from jax import lax
from jax.experimental import pallas as pl
from jax.experimental.pallas import tpu as pltpu
from jax.sharding import PartitionSpec as P

MESH = pl.DeviceIdType.MESH
LANES = 128
SUB = 8
ITERS = 3
SWEEPS = 4 * ITERS + 2


def kernel(
    ntm, nsp, reach, f_hbm, k_hbm, out_hbm,
    fstage, kloc, kstage, fwin, kwin, scl, inv, gn, gs, gw, ge, taus, abufs, bbufs, qs, last, ends, res, part, red,
    f_sem, k_sem, r_sem, o_sem, own_sem,
):
    n = ntm * nsp
    mt, ms = lax.axis_index("tm"), lax.axis_index("space")
    me = mt * nsp + ms
    tl, nb, own, rows, _ = f_hbm.shape
    steps, width = fwin.shape[0], fwin.shape[1]
    strips = nsp // 2
    half, ml = ms // strips, ms % strips
    mb = mt * strips + ml
    nx = scl.shape[1] - 2 * SUB
    groups, owned = nx // SUB, strips * rows // SUB
    spare = groups - owned
    edge = jnp.where(half == 0, ml >= strips - reach, ml < reach)

    def place(s, side):
        at = s - side * (strips - reach)
        return pl.ds(pl.multiple_of(SUB + at * rows, SUB), rows)

    def send(src, dst, sem, arrival, dt, ds):
        return pltpu.make_async_remote_copy(
            src_ref=src, dst_ref=dst, send_sem=sem, recv_sem=arrival,
            device_id=(dt, ds), device_id_type=MESH)

    def f_copy(dt, side, dl):
        return send(fstage.at[:, dt * strips + dl],
                    fwin.at[pl.ds(mt * tl, tl), :, place(ms, side)],
                    f_sem.at[0], f_sem.at[1], dt, side * strips + dl)

    def f_cross(dt, side, dl):
        return send(fstage.at[:, dt * strips + dl],
                    fwin.at[pl.ds(mt * tl, tl), :, place(ms, side)],
                    f_sem.at[0], f_sem.at[2], dt, side * strips + dl)

    def k_copy(side, dl):
        return send(kstage.at[dl], kwin.at[:, place(ms, side)],
                    k_sem.at[0], k_sem.at[1], mt, side * strips + dl)

    def r_copy(dt, ds):
        return send(part, red.at[me], r_sem.at[0], r_sem.at[1], dt, ds)

    def res_piece(dt, dl):
        return res.at[pl.ds(dt * tl, tl), :, pl.ds(pl.multiple_of(dl * rows, SUB), rows)]

    def o_copy(dt, dl):
        return send(res_piece(dt, dl), out_hbm.at[:, pl.ds(mb * own, own)],
                    o_sem.at[0], o_sem.at[1], dt, half * strips + dl)

    def await_bytes(ref, sem):
        pltpu.make_async_copy(ref, ref, sem).wait()

    def loop(low, high, act):
        def step(j, carry):
            act(j)
            return carry
        lax.fori_loop(low, high, step, 0)

    def turn(at, by, size):
        moved = at + by
        return jnp.where(moved >= size, moved - size, moved)

    def peers(act):
        for js in sorted(range(nsp), key=lambda j: abs(j - nsp // 2)):
            ds = turn(ms, js, nsp)
            for jt in range(ntm):
                if js or jt:
                    act(turn(mt, jt, ntm), ds)

    def home(i):
        return 2 * turn(ml // 2, 1 + i // 2, strips // 2) + (ml + i) % 2

    def mates(act):
        for i in range(strips):
            for jt in range(ntm):
                if (i, jt) != (strips - 2, 0):
                    act(turn(mt, jt, ntm), half, home(i))

    def across(i):
        near = 2 * (i // 2)
        return jnp.where(half == 0, near, strips - 2 - near) + (ml + i) % 2

    def others(act):
        for i in range(strips):
            for jt in range(ntm):
                act(turn(mt, jt, ntm), 1 - half, across(i))

    barrier = pltpu.get_barrier_semaphore()
    peers(lambda dt, ds: pl.semaphore_signal(
        barrier, inc=1, device_id=(dt, ds), device_id_type=MESH))
    loads = [
        pltpu.make_async_copy(f_hbm, fstage.at[:, :, pl.ds(0, own)], own_sem.at[0]),
        pltpu.make_async_copy(k_hbm, kloc, own_sem.at[1]),
        pltpu.make_async_copy(
            k_hbm.at[pl.ds(mt * strips, strips)], kstage.at[:, pl.ds(0, own)], own_sem.at[2]),
    ]
    for load in loads:
        load.start()
    lane = lax.broadcasted_iota(jnp.int32, (SUB, LANES), 1)
    first, final, ahead = lane == 0, lane == LANES - 1, lane < LANES // 2

    def beside(d, right, left):
        return jnp.where(ahead, right * jnp.where(d < nb - 1, 1.0, 0.0),
                         left * jnp.where(d > 0, 1.0, 0.0))

    def after(d):
        return jnp.minimum(d + 1, nb - 1)

    def before(d):
        return jnp.maximum(d - 1, 0)

    for load in loads:
        load.wait()

    def interleave(act):
        by = 1
        while by < own:
            odd = (lane & by) != 0

            def swap(tiles, by=by, odd=odd):
                pairs = [(c, c + by) for c in range(own) if not c & by]
                got = [[(get(a), get(b)) for a, b in pairs] for get, _ in tiles]
                turned = [[(pltpu.roll(y, by, 1), pltpu.roll(x, LANES - by, 1)) for x, y in g] for g in got]
                for (_, put), g, h in zip(tiles, got, turned):
                    for (a, b), (x, y), (ry, rx) in zip(pairs, g, h):
                        put(a, jnp.where(odd, ry, x))
                        put(b, jnp.where(odd, y, rx))

            act(swap, by == 1)
            by *= 2

    def overlap_k(s):
        d = mt * strips + s
        for r in range(0, rows, SUB):
            kstage[s, own, r:r + SUB, :] = beside(
                d, kloc[after(d), 0, r:r + SUB, :], kloc[before(d), own - 1, r:r + SUB, :])

    def overlap_f(d):
        for t in range(tl):
            for r in range(0, rows, SUB):
                fstage[t, d, own, r:r + SUB, :] = beside(
                    d, fstage[t, after(d), 0, r:r + SUB, :],
                    fstage[t, before(d), own - 1, r:r + SUB, :])

    def cell(ref, *head, r=0):
        def get(c):
            return ref[(*head, c, pl.ds(r, SUB), slice(None))]

        def put(c, x):
            ref[(*head, c, pl.ds(r, SUB), slice(None))] = x
        return get, put

    batch = 4 if nb % 4 == 0 else 1
    bands = range(0, rows, SUB)

    def weave_k(swap, _):
        swap([cell(kstage, s, r=r) for s in range(strips) for r in bands])

    def weave_f(swap, _):
        loop(0, nb // batch, lambda j: swap(
            [cell(fstage, t, batch * j + d, r=r) for d in range(batch) for t in range(tl) for r in bands]))

    loop(0, strips, overlap_k)
    interleave(weave_k)
    loop(0, nb, overlap_f)
    interleave(weave_f)
    own_k = pltpu.make_async_copy(kstage.at[ml], kwin.at[:, place(ms, half)], k_sem.at[1])
    own_f = pltpu.make_async_copy(
        fstage.at[:, mb], fwin.at[pl.ds(mt * tl, tl), :, place(ms, half)], f_sem.at[1])
    zero = jnp.zeros((SUB, LANES), jnp.float32)
    rims = (slice(0, SUB), slice(SUB + nx, SUB + nx + SUB))

    def clear(c):
        for rim in rims:
            kwin[c, rim, :] = zero
            scl[c, rim, :] = zero
            for s in range(steps):
                last[s, c, rim, :] = zero
                for many in (taus, abufs, bbufs, qs):
                    for j in range(many.shape[0]):
                        many[j, s, c, rim, :] = zero

    loop(0, width, clear)
    pl.semaphore_wait(barrier, n - 1)

    for i in range(strips):
        if i != strips - 2:
            k_copy(half, home(i)).start()

    @pl.when(edge)
    def _():
        for i in range(strips):
            k_copy(1 - half, across(i)).start()

    mates(lambda *to: f_copy(*to).start())

    @pl.when(edge)
    def _():
        others(lambda *to: f_cross(*to).start())

    own_k.start()
    own_f.start()
    await_bytes(kwin.at[:, pl.ds(SUB, nx)], k_sem.at[1])

    def turned(x0, x1, rim):
        down, up = pltpu.roll(rim, 1, 1), pltpu.roll(rim, LANES - 1, 1)
        start = jnp.where(lane < own, pltpu.roll(x1, own + 1, 1), pltpu.roll(x1, own, 1))
        end = jnp.where(lane >= LANES - own,
                        pltpu.roll(x0, LANES - own - 1, 1), pltpu.roll(x0, LANES - own, 1))
        return (jnp.where(first, down, start), jnp.where(first, pltpu.roll(x1, 1, 1), down),
                jnp.where(final, up, end), jnp.where(final, pltpu.roll(x0, LANES - 1, 1), up))

    def lefts(xs):
        ends = turned(xs[0], xs[own - 1], xs[own])
        return [ends[0], *xs[:own - 1], ends[1]]

    def rights(xs):
        ends = turned(xs[0], xs[own - 1], xs[own])
        return [*xs[1:own], ends[2], ends[3]]

    def near(p, offset):
        return pl.ds(SUB + p + offset, SUB)

    def at(p):
        return pl.ds(SUB + p, SUB)

    def flat(p):
        return pl.ds(p, SUB)

    def by_group(act):
        return lambda i: act(pl.multiple_of(SUB * i, SUB))

    inside = beside(mb, jnp.ones((SUB, LANES), jnp.float32), jnp.ones((SUB, LANES), jnp.float32))

    def weights_first(i):
        ks = [kwin[c, at(i), :] for c in range(width)]
        for c, (k, l, r) in enumerate(zip(ks, lefts(ks), rights(ks))):
            up, down = kwin[c, near(i, -1), :], kwin[c, near(i, 1), :]
            diag = 1.0 + 0.5 * (k + up) + 0.5 * (k + down) + 0.5 * (k + l) + 0.5 * (k + r)
            scale = 1.0 / jnp.sqrt(diag)
            scl[c, at(i), :] = scale * inside if c == own else scale
            inv[c, flat(i), :] = 1.0 / diag

    def weights_second(i):
        ks = [kwin[c, at(i), :] for c in range(width)]
        ss = [scl[c, at(i), :] for c in range(width)]
        quads = zip(ks, lefts(ks), rights(ks), ss, lefts(ss), rights(ss))
        for c, (k, kl, kr, s, sl, sr) in enumerate(quads):
            half_s = 0.5 * s
            gn[c, flat(i), :] = half_s * (k + kwin[c, near(i, -1), :]) * scl[c, near(i, -1), :]
            gs[c, flat(i), :] = half_s * (k + kwin[c, near(i, 1), :]) * scl[c, near(i, 1), :]
            gw[c, flat(i), :] = half_s * (k + kl) * sl
            ge[c, flat(i), :] = half_s * (k + kr) * sr

    loop(0, groups, by_group(weights_first))
    loop(0, groups, by_group(weights_second))

    def start_of(row):
        return jnp.where(half == 0, row, nx - SUB - row)

    down_rows = lax.broadcasted_iota(jnp.int32, (SUB, LANES), 0)
    inwards = jnp.where(half == 0, down_rows, SUB - 1 - down_rows)

    def scale_in(j):
        i = pl.multiple_of(start_of(SUB * j), SUB)
        for c in range(width):
            s = scl[c, at(i), :]
            for t in range(steps):
                taus[0, t, c, at(i), :] = s * fwin[steps - 1 - t, c, at(i), :]

    def turn_ends(src, firsts):
        for j, row in enumerate(firsts):
            i = start_of(row)
            for t in range(steps):
                cells = turned(src[t, 0, at(i), :], src[t, own - 1, at(i), :], src[t, own, at(i), :])
                for e, x in enumerate(cells):
                    ends[j, t, e] = x

    def sweep(src, use):
        def block(j, row, total, counted):
            i = start_of(row)
            for c in range(width):
                wn, wso = gn[c, flat(i), :], gs[c, flat(i), :]
                ww, we = gw[c, flat(i), :], ge[c, flat(i), :]
                out = []
                for t in range(steps):
                    left = ends[j, t, 0] if c == 0 else ends[j, t, 1] if c == own else src[t, c - 1, at(i), :]
                    right = (ends[j, t, 2] if c == own - 1 else ends[j, t, 3] if c == own
                             else src[t, c + 1, at(i), :])
                    out.append(
                        wn * src[t, c, near(i, -1), :] + wso * src[t, c, near(i, 1), :]
                        + (ww * left + we * right))
                term = use(c, i, [src[t, c, at(i), :] for t in range(steps)], out)
                if term is not None and c < own and counted > 0:
                    total = total + (term if counted >= SUB else jnp.where(inwards < counted, term, 0.0))
            return total
        return block

    def one(it):
        def use(c, i, x, g):
            for t in range(steps):
                abufs[it, t, c, at(i), :] = x[t] + g[t]
        return taus.at[it], use

    def two(it):
        def use(c, i, x, g):
            for t in range(steps):
                bbufs[it, t, c, at(i), :] = 0.25 * taus[it, t, c, at(i), :] + g[t]
        return abufs.at[it], use

    def three(it):
        def use(c, i, x, g):
            term = zero
            for t in range(steps):
                v = taus[it, t, c, at(i), :]
                y = 1.5 * v + g[t]
                qs[it, t, c, at(i), :] = y
                term = term + v * y
            return term
        return bbufs.at[it], use

    def operate(it):
        def use(c, i, x, g):
            shrink = inv[c, flat(i), :]
            term = zero
            for t in range(steps):
                y = x[t] - g[t]
                if t:
                    y = y - shrink * x[t - 1]
                taus[it + 1, steps - 1 - t, c, at(i), :] = y
                term = term + y * x[steps - 1 - t]
            return term
        return qs.at[it], use

    def norm_one(c, i, x, g):
        term = zero
        for t in range(steps):
            last[t, c, at(i), :] = g[t]
            term = term + (x[t] * (1.5 * x[t] + 0.25 * g[t]) + g[t] * g[t])
        return term

    def norm_two(c, i, x, g):
        term = zero
        for t in range(steps):
            term = term + x[t] * g[t]
        return term

    plan = []
    for it in range(ITERS):
        plan += [(*one(it), None), (*two(it), None),
                 (*three(it), 2 * it - 1 if it else None), (*operate(it), 2 * it)]
    plan += [(taus.at[ITERS], norm_one, 2 * ITERS - 1), (last, norm_two, 2 * ITERS - 1)]
    moments = [zero] * (2 * ITERS)

    def run(number, firsts, counted, looped=0):
        src, use, slot = plan[number - 1]
        turn_ends(src, firsts)
        block = sweep(src, use)
        total = zero if slot is None else moments[slot]
        if looped:
            total = lax.fori_loop(0, looped, lambda j, acc: block(j, SUB * j, acc, SUB), total)
        for j in range(looped, len(firsts)):
            total = block(j, firsts[j], total, counted - SUB * j)
        if slot is not None:
            moments[slot] = total

    def up_to(count):
        return -(-count // SUB)

    inner = owned * SUB

    await_bytes(fwin.at[:, :, pl.ds(SUB, inner)], f_sem.at[1])
    loop(0, owned, scale_in)
    for j in range(1, SWEEPS + 1):
        run(j, [SUB * i for i in range(up_to(inner - j))], inner - j, (inner - j) // SUB)
    await_bytes(fwin.at[:, :, pl.ds(SUB, nx - inner)], f_sem.at[2])
    loop(owned, groups, scale_in)
    for j in range(1, SWEEPS + 1):
        run(j, [inner - j + SUB * i for i in range(up_to(SWEEPS))], j)

    row = jnp.zeros((1, LANES), jnp.float32)
    lane1 = lax.broadcasted_iota(jnp.int32, (1, LANES), 1)
    for j, m in enumerate(moments):
        value = jnp.sum(jnp.sum(m, axis=0, keepdims=True), axis=1, keepdims=True)
        row = jnp.where(lane1 == j, value, row)
    part[...] = row
    red[me] = row
    peers(lambda dt, ds: r_copy(dt, ds).start())

    def scaled(l, t, it, begin):
        i = pl.multiple_of(SUB * (l + half * spare), SUB)

        def get(c):
            q = qs[it, t, c, at(i), :]
            return scl[c, at(i), :] * q if begin else q

        def put(c, x):
            qs[it, t, c, at(i), :] = x
        return get, put

    def unweave(swap, begin):
        loop(0, owned, lambda l: [
            swap([scaled(l, t, it, begin) for t in range(steps)]) for it in range(ITERS)] and None)

    interleave(unweave)
    await_bytes(red.at[pl.ds(0, n - 1)], r_sem.at[1])
    total = lax.fori_loop(0, n, lambda j, acc: acc + red[j], jnp.zeros((1, LANES), jnp.float32))
    n1, n2, n3, n4, n5, n6 = [
        jnp.sum(jnp.where(lane1 == j, total, 0.0), axis=1, keepdims=True) for j in range(6)]

    tiny = 1e-7
    d1 = jnp.maximum(n2, 1e-37)
    l21, l31 = n3 / d1, n4 / d1
    d2 = jnp.maximum(n4 - l21 * n3, jnp.maximum(tiny * n4, 1e-37))
    e32 = n5 - l31 * n3
    l32 = e32 / d2
    d3 = jnp.maximum(n6 - l31 * n4 - l32 * e32, jnp.maximum(tiny * n6, 1e-37))
    y2 = n2 - l21 * n1
    y3 = n3 - l31 * n1 - l32 * y2
    a2 = y3 / d3
    a1 = y2 / d2 - l32 * a2
    a0 = n1 / d1 - l21 * a1 - l31 * a2

    def finish(l):
        i = pl.multiple_of(SUB * (l + half * spare), SUB)
        for c in range(own):
            for t in range(steps):
                res[t, c, pl.ds(pl.multiple_of(SUB * l, SUB), SUB), :] = (
                    a0 * qs[0, t, c, at(i), :] + a1 * qs[1, t, c, at(i), :]
                    + a2 * qs[2, t, c, at(i), :])

    own_out = pltpu.make_async_copy(
        res_piece(mt, ml), out_hbm.at[:, pl.ds(mb * own, own)], o_sem.at[1])
    for i in range(strips):
        dl = home(i)
        for r in range(rows // SUB):
            finish(dl * (rows // SUB) + r)
        for jt in range(ntm):
            if (i, jt) == (strips - 2, 0):
                own_out.start()
            else:
                o_copy(turn(mt, jt, ntm), dl).start()
    await_bytes(kstage.at[pl.ds(0, strips - 1)], k_sem.at[0])
    await_bytes(fstage.at[:, pl.ds(0, nb - 1)], f_sem.at[0])

    @pl.when(edge)
    def _():
        await_bytes(kstage, k_sem.at[0])
        await_bytes(fstage, f_sem.at[0])

    await_bytes(red.at[pl.ds(0, n - 1)], r_sem.at[0])
    await_bytes(out_hbm, o_sem.at[1])
    await_bytes(out_hbm.at[:, pl.ds(0, (nb - 1) * own)], o_sem.at[0])


def solution(mesh):
    ntm, nsp = mesh.shape["tm"], mesh.shape["space"]
    n, nb = ntm * nsp, ntm * (nsp // 2)

    def body(forcing, conductivity):
        tl, rows, columns = forcing.shape
        tiles = columns // LANES
        own = tiles // nb
        width = own + 1
        reach = -(-(SWEEPS + 1) // rows)
        steps, nx = tl * ntm, (nsp // 2 + reach) * rows
        f = forcing.reshape(tl, rows, nb, own, LANES).transpose(0, 2, 3, 1, 4)
        k = conductivity.reshape(rows, nb, own, LANES).transpose(1, 2, 0, 3)
        padded = pltpu.VMEM((width, nx + 2 * SUB, LANES), jnp.float32)
        plain = pltpu.VMEM((width, nx, LANES), jnp.float32)

        def fields(*many):
            return pltpu.VMEM((*many, steps, width, nx + 2 * SUB, LANES), jnp.float32)

        dma = pltpu.SemaphoreType.DMA
        f, k = (pltpu.with_memory_space_constraint(x, pltpu.HBM) for x in (f, k))
        out = pl.pallas_call(
            functools.partial(kernel, ntm, nsp, reach),
            out_shape=jax.ShapeDtypeStruct((tl, tiles, rows, LANES), jnp.float32),
            in_specs=[pl.BlockSpec(memory_space=pltpu.HBM)] * 2,
            out_specs=pl.BlockSpec(memory_space=pl.ANY),
            scratch_shapes=[
                pltpu.VMEM((tl, nb, width, rows, LANES), jnp.float32),
                pltpu.VMEM((nb, own, rows, LANES), jnp.float32),
                pltpu.VMEM((nsp // 2, width, rows, LANES), jnp.float32),
                fields(), padded, padded, plain, plain, plain, plain, plain,
                fields(ITERS + 1), fields(ITERS), fields(ITERS), fields(ITERS), fields(),
                pltpu.VMEM((nx // SUB, steps, 4, SUB, LANES), jnp.float32),
                pltpu.VMEM((steps, own, nsp // 2 * rows, LANES), jnp.float32),
                pltpu.VMEM((1, LANES), jnp.float32),
                pltpu.VMEM((n, 1, LANES), jnp.float32),
                dma((3,)), dma((2,)), dma((2,)), dma((2,)), dma((3,)),
            ],
            compiler_params=pltpu.CompilerParams(
                collective_id=0, has_side_effects=True, vmem_limit_bytes=40 * 1024 * 1024),
        )(f, k)
        return out.transpose(0, 2, 1, 3).reshape(tl, rows, columns)

    return jax.shard_map(
        body,
        mesh=mesh,
        in_specs=(P("tm", "space", None), P("space", None)),
        out_specs=P("tm", "space", None),
        check_vma=False,
    )
```
